32 devices in a mesh: ctx: 8 (over z, x), fsdp: 4 (over y, core).
Axes of the slice: x: 2, y: 2, z: 4, core: 2. Of those that a mesh axis runs over, the one named last changes fastest.
Arguments:
- hidden_states: bfloat16 [4, 2048, 2048], P('fsdp', 'ctx'), may hold values from -8 to 8
- positions: int32 [2048], replicated, may hold values from 0 to 2047, as said below
- ln1_gain: bfloat16 [2048], P('fsdp'), may hold values from 0.5 to 1.5
- ln1_bias: bfloat16 [2048], P('fsdp'), may hold values from -3 to 3
- ln2_gain: bfloat16 [2048], P('fsdp'), may hold values from 0.5 to 1.5
- ln2_bias: bfloat16 [2048], P('fsdp'), may hold values from -3 to 3
- qkv_weight: bfloat16 [2048, 6144], P(None, 'fsdp'), may hold values from -0.26516504 to 0.26516504
- qkv_bias: bfloat16 [6144], P('fsdp'), may hold values from -3 to 3
- out_weight: bfloat16 [2048, 2048], P(None, 'fsdp'), may hold values from -2 to 2
- out_bias: bfloat16 [2048], P('fsdp'), may hold values from -3 to 3
- up_weight: bfloat16 [2048, 8192], P(None, 'fsdp'), may hold values from -0.125 to 0.125
- up_bias: bfloat16 [8192], P('fsdp'), may hold values from -3 to 3
- down_weight: bfloat16 [8192, 2048], P(None, 'fsdp'), may hold values from -0.0625 to 0.0625
- down_bias: bfloat16 [2048], P('fsdp'), may hold values from -3 to 3
- grad_output: bfloat16 [4, 2048, 2048], P('fsdp', 'ctx'), may hold values from -6 to 6
Outputs:
- output: bfloat16 [4, 2048, 2048], P('fsdp', 'ctx')
- grad_input: bfloat16 [4, 2048, 2048], P('fsdp', 'ctx')
- grad_ln1_gain: float32 [2048], P('fsdp')
- grad_ln1_bias: float32 [2048], P('fsdp')
- grad_ln2_gain: float32 [2048], P('fsdp')
- grad_ln2_bias: float32 [2048], P('fsdp')
- grad_qkv_weight: float32 [2048, 6144], P(None, 'fsdp')
- grad_qkv_bias: float32 [6144], P('fsdp')
- grad_out_weight: float32 [2048, 2048], P(None, 'fsdp')
- grad_out_bias: float32 [2048], P('fsdp')
- grad_up_weight: float32 [2048, 8192], P(None, 'fsdp')
- grad_up_bias: float32 [8192], P('fsdp')
- grad_down_weight: float32 [8192, 2048], P(None, 'fsdp')
- grad_down_bias: float32 [2048], P('fsdp')
The draws below stay inside these ranges and needn't reach their ends.
Inputs may be any that keep to these rules, and one draw needn't show every extreme that they name: Each device's 256 stored tokens are two runs of 128 consecutive positions: half-block j of the sequence and its mirror half-block 2 * 8 - 1 - j, in either order; over all devices every position appears once.
All inputs are finite; a program needn't handle non-finite values.
Results may differ from the reference program's by a relative error of at most 0.019.
Values may be sent and summed in bfloat16 or wider, within the bound.
No kernel may reach another device: no remote copies, remote signals or barrier semaphores. Data moves between devices by JAX's collectives and lax.ppermute only.
A program may use at most 640 MiB of HBM per device.

```python
import math
import jax
import jax.numpy as jnp
from jax import lax

D = 2048
HEADS = 8
HEAD = 256
ROT = 64
FF = 8192
BLK = 256
LEN = 2048
SEQS = 4


def draw_hidden_states(key, part):
    base = jax.random.normal(jax.random.fold_in(key, 11), (SEQS, LEN, D), jnp.float32)
    return jnp.clip(base, -6.0, 6.0).astype(jnp.bfloat16)


def draw_qkv_weight(key, part):
    limit = 12.0 / D ** 0.5
    weight = jax.random.normal(jax.random.fold_in(key, 21), (D, 3 * D), jnp.float32) / D ** 0.5
    return jnp.clip(weight, -limit, limit).astype(jnp.bfloat16)


def draw_positions(key, part):
    block_count = LEN // BLK
    halfway = BLK // 2
    pairing = jax.random.permutation(jax.random.fold_in(key, 31), block_count).astype(jnp.int32)
    flipped = jax.random.randint(jax.random.fold_in(key, 32), (block_count,), 0, 2)
    mirror = 2 * block_count - 1 - pairing
    first_half = jnp.where(flipped == 1, mirror, pairing)
    second_half = jnp.where(flipped == 1, pairing, mirror)
    within = jnp.arange(halfway, dtype=jnp.int32)
    joined = jnp.concatenate([first_half[:, None] * halfway + within[None, :], second_half[:, None] * halfway + within[None, :]], axis=1)
    return joined.reshape(LEN).astype(jnp.int32)


def steps_of(rng, shape, split, least, largest):
    gain = 1.0
    for position, shards_of in split:
        heights = jax.random.uniform(jax.random.fold_in(jax.random.fold_in(rng, 6), position), (shards_of,), jnp.float32, least / len(split), largest / len(split))
        gain = gain * jnp.repeat(jnp.exp(heights), shape[position] // shards_of).reshape((-1,) + (1,) * (len(shape) - 1 - position))
    return gain


def noise(stream_key, extent, scale, most, cuts=(), kind=jnp.bfloat16):
    loudness = steps_of(stream_key, extent, cuts, -0.22, 0.18) if cuts else 1.0
    values = jax.random.normal(stream_key, extent, jnp.float32) * scale * loudness
    return jnp.minimum(jnp.maximum(values, -most), most).astype(kind)


def setup_inputs(seed: int = 0) -> dict:
    keys = jax.random.split(jax.random.key(seed), 16)
    return {
        "hidden_states": draw_hidden_states(jax.random.fold_in(keys[15], 71), 0),
        "positions": draw_positions(jax.random.fold_in(keys[15], 71), 0),
        "ln1_gain": jnp.clip(1.0 + 0.1 * jax.random.normal(keys[2], (D,), jnp.float32), 0.5, 1.5).astype(jnp.bfloat16),
        "ln1_bias": noise(keys[3], (D,), 0.5, 3.0, ((0, 4),)),
        "ln2_gain": jnp.clip(1.0 + 0.1 * jax.random.normal(keys[4], (D,), jnp.float32), 0.5, 1.5).astype(jnp.bfloat16),
        "ln2_bias": noise(keys[5], (D,), 0.5, 3.0, ((0, 4),)),
        "qkv_weight": draw_qkv_weight(jax.random.fold_in(keys[15], 71), 0),
        "qkv_bias": noise(keys[7], (3 * D,), 0.5, 3.0, ((0, 4),)),
        "out_weight": noise(keys[8], (D, D), 8 ** -0.5, 2.0, ((1, 4),)),
        "out_bias": noise(keys[9], (D,), 0.5, 3.0, ((0, 4),)),
        "up_weight": noise(keys[10], (D, FF), D ** -0.5, 0.125, ((1, 4),)),
        "up_bias": noise(keys[11], (FF,), 0.5, 3.0, ((0, 4),)),
        "down_weight": noise(keys[12], (FF, D), FF ** -0.5, 0.0625, ((1, 4),)),
        "down_bias": noise(keys[13], (D,), 0.5, 3.0, ((0, 4),)),
        "grad_output": noise(keys[14], (SEQS, LEN, D), 1.0, 6.0, ((0, 4), (1, 8))),
    }


@jax.custom_vjp
def low(v):
    return lax.optimization_barrier(v.astype(jnp.bfloat16)).astype(jnp.float32)

@jax.custom_vjp
def low_back(v):
    return v

def low_keep(v):
    return (low(v), None)

def low_pass(kept, grad):
    return (grad,)

def back_keep(v):
    return (v, None)

def back_low(kept, grad):
    return (low(grad),)
low.defvjp(low_keep, low_pass)
low_back.defvjp(back_keep, back_low)
EPSILON = 1e-05
HIGHEST = lax.Precision.HIGHEST

def matmul_high(left, right):
    return jnp.dot(left, right, preferred_element_type=jnp.float32, precision=HIGHEST)

def layer_norm(values, gain_vec, shift_vec):
    centre = lax.optimization_barrier(jnp.mean(values, axis=-1, keepdims=True))
    offsets = values - centre
    spread = lax.optimization_barrier(jnp.mean(offsets * offsets, axis=-1, keepdims=True))
    return offsets * lax.rsqrt(spread + EPSILON) * gain_vec + shift_vec

def rotate(tensor, places):
    halfway = ROT // 2
    frequency = jnp.exp(jnp.arange(halfway, dtype=jnp.float32) * (-2.0 * math.log(10000.0) / ROT))
    angles = places.astype(jnp.float32)[:, None] * frequency[None, :]
    cosine = jnp.cos(angles)[:, None, :]
    sine_table = jnp.sin(angles)[:, None, :]
    first_part = tensor[..., :halfway]
    second_part = tensor[..., halfway:ROT]
    return jnp.concatenate([first_part * cosine - second_part * sine_table, second_part * cosine + first_part * sine_table, tensor[..., ROT:]], axis=-1)

def forward_seq(seq_rows, param_set, places):
    ln1_gain, ln1_bias, ln2_gain, ln2_bias, qkv_weight, qkv_bias, out_weight, out_bias, up_weight, up_bias, down_weight, down_bias = param_set
    length = seq_rows.shape[0]
    normed_one = low(layer_norm(seq_rows, ln1_gain, ln1_bias))
    mixed_rows = low_back(matmul_high(normed_one, qkv_weight) + qkv_bias)
    queries = low(rotate(mixed_rows[:, :D].reshape(length, HEADS, HEAD), places))
    key_rows = low(rotate(mixed_rows[:, D:2 * D].reshape(length, HEADS, HEAD), places))
    value_rows = low(mixed_rows[:, 2 * D:].reshape(length, HEADS, HEAD))
    block_rows = math.gcd(length, 1024)
    block_count = length // block_rows

    def attend(inputs_pair):
        query_block, query_places = inputs_pair
        scores = jnp.einsum('qhd,khd->hqk', query_block, key_rows, precision=HIGHEST) * HEAD ** (-0.5)
        visible = places[None, :] <= query_places[:, None]
        scores = low_back(jnp.where(visible[None], scores, -1e+30))
        weights = low(jax.nn.softmax(scores, axis=-1))
        return jnp.einsum('hqk,khd->qhd', weights, value_rows, precision=HIGHEST)
    attended = lax.map(jax.checkpoint(attend), (queries.reshape(block_count, block_rows, HEADS, HEAD), places.reshape(block_count, block_rows)))
    attended = low_back(low(attended.reshape(length, D)))
    attn_result = matmul_high(attended, out_weight) + out_bias
    normed_two = low(layer_norm(seq_rows, ln2_gain, ln2_bias))
    up_in = low_back(matmul_high(normed_two, up_weight) + up_bias)
    activated = low(jax.nn.gelu(up_in, approximate=False))
    mlp_result = matmul_high(activated, down_weight) + down_bias
    return seq_rows + attn_result + mlp_result

def reference(hidden_states, positions, ln1_gain, ln1_bias, ln2_gain, ln2_bias, qkv_weight, qkv_bias, out_weight, out_bias, up_weight, up_bias, down_weight, down_bias, grad_output):
    param_set = tuple((p_item.astype(jnp.float32) for p_item in (ln1_gain, ln1_bias, ln2_gain, ln2_bias, qkv_weight, qkv_bias, out_weight, out_bias, up_weight, up_bias, down_weight, down_bias)))
    initial = tuple((jnp.zeros(p_item.shape, jnp.float32) for p_item in param_set))

    def per_sequence(running, inputs_pair):
        seq_rows, cotangent = inputs_pair
        result, pullback = jax.vjp(lambda state_in, params_in: forward_seq(state_in, params_in, positions), seq_rows.astype(jnp.float32), param_set)
        grad_rows, grad_params = pullback(cotangent.astype(jnp.float32))
        running = jax.tree.map(lambda summed, added: summed + added, running, grad_params)
        return (running, (result.astype(jnp.bfloat16), grad_rows.astype(jnp.bfloat16)))
    running, (outputs, grad_rows) = lax.scan(per_sequence, initial, (hidden_states, grad_output))
    return (outputs, grad_rows, running[0], running[1], running[2], running[3], running[4], running[5], running[6], running[7], running[8], running[9], running[10], running[11])
```

```python
import functools
import math

import jax
import jax.numpy as jnp
from jax import lax
from jax.experimental import pallas as pl
from jax.experimental.pallas import tpu as pltpu
from jax.sharding import PartitionSpec as P

HEADS = 8
HEAD = 256
ROT = 64
LANES = 128

EPSILON = 1e-05
INV_ROOT_TWO = 0.7071067811865476
INV_ROOT_TAU = 0.3989422804014327

F32 = jnp.float32
BF16 = jnp.bfloat16


def partner(block, bits):
    size = lax.axis_size("fsdp")
    return lax.ppermute(block, "fsdp", [(i, i ^ bits) for i in range(size)])


def gather_by_partner(block):
    across = partner(block, 2)
    beside = partner(block, 1)
    return jnp.stack([block, beside, across, partner(across, 1)])


def exchange_by_partner(pieces):
    return [pieces[0]] + [partner(pieces[bits], bits) for bits in range(1, len(pieces))]


def scatter_sum_by_partner(parts):
    beside = partner(jnp.stack([parts[1], parts[3]]).astype(BF16), 1)
    across = partner((parts[2] + beside[1].astype(F32)).astype(BF16), 2)
    return parts[0] + beside[0].astype(F32) + across.astype(F32)


def ring_order(size):
    return list(range(0, size, 2)) + list(range(size - 1 - size % 2, 0, -2))


def hop(block, distance):
    order = ring_order(lax.axis_size("ctx"))
    size = len(order)
    return lax.ppermute(
        block, "ctx", [(order[p], order[(p + distance) % size]) for p in range(size)]
    )


def ring_place():
    order = ring_order(lax.axis_size("ctx"))
    place = [order.index(i) for i in range(len(order))]
    return jnp.asarray(place, jnp.int32)[lax.axis_index("ctx")]


def ring_sum(make, place):
    size = lax.axis_size("ctx")
    far = size // 2

    def chunk(shift):
        return make(jnp.mod(place + shift, size))

    far_chunk = chunk(far).astype(BF16)
    half = far_chunk.shape[1] // 2
    ahead = hop(far_chunk[:, :half], 1)
    behind = hop(far_chunk[:, half:], -1)

    def widen_ahead(part):
        part = part.astype(F32)
        return part if part.shape[1] == 2 * half else jnp.pad(part, ((0, 0), (0, half)))

    def widen_behind(part):
        part = part.astype(F32)
        return part if part.shape[1] == 2 * half else jnp.pad(part, ((0, 0), (half, 0)))

    for shift in range(far - 1, 0, -1):
        ahead = hop((chunk(shift) + widen_ahead(ahead)).astype(BF16), 1)
        behind = hop((chunk(-shift) + widen_behind(behind)).astype(BF16), -1)
    return chunk(0) + widen_ahead(ahead) + widen_behind(behind)


def ring_spread(own):
    far = lax.axis_size("ctx") // 2
    half = own.shape[-1] // 2
    parts = [(0, 0, own)]
    ahead = behind = own
    for shift in range(1, far):
        ahead = hop(ahead, 1)
        behind = hop(behind, -1)
        parts += [(-shift, 0, ahead), (shift, 0, behind)]
    ahead = hop(ahead[..., :half], 1)
    behind = hop(behind[..., half:], -1)
    return parts + [(far, 0, ahead), (far, half, behind)]


def assemble_kernel(shifts, firsts, cycle, split, place_ref, *refs):
    count = len(shifts)
    parts, out_ref = refs[:count], refs[count]
    narrow, wide, in_sem, out_sem = refs[count + 1 :]

    def columns(i):
        return pl.ds(0, parts[i].shape[-1])

    def fetch(i):
        slot = i % 2
        return pltpu.make_async_copy(
            parts[i], narrow.at[slot, ..., columns(i)], in_sem.at[slot]
        )

    def put(i):
        slot = i % 2
        index = lax.rem(place_ref[0] + (shifts[i] + cycle), cycle)
        target = pl.ds(firsts[i], parts[i].shape[-1])
        to = out_ref.at[:, index, :, target] if split else out_ref.at[index, :, target]
        return pltpu.make_async_copy(wide.at[slot, ..., columns(i)], to, out_sem.at[slot])

    fetch(0).start()
    for i in range(count):
        slot = i % 2
        if i + 1 < count:
            fetch(i + 1).start()
        fetch(i).wait()
        if i >= 2:
            put(i - 2).wait()
        rows = narrow.shape[-2]
        step = math.gcd(rows, 64)

        @pl.loop(0, rows // step)
        def _(block):
            some = pl.ds(pl.multiple_of(block * step, step), step)
            if split:
                for which in range(narrow.shape[1]):
                    wide[slot, which, some, :] = narrow[slot, which, some, :].astype(F32)
            else:
                wide[slot, some, :] = narrow[slot, some, :].astype(F32)

        put(i).start()
    for i in range(max(count - 2, 0), count):
        put(i).wait()


def assemble(parts, place, name):
    cycle = lax.axis_size("ctx")
    shifts = tuple(shift for shift, _, _ in parts)
    firsts = tuple(first for _, first, _ in parts)
    chunks = [piece for _, _, piece in parts]
    shape = chunks[0].shape
    split = len(shape) == 3
    out_shape = (shape[0], cycle) + shape[1:] if split else (cycle,) + shape
    anywhere = pl.BlockSpec(memory_space=pl.ANY)
    return pl.pallas_call(
        functools.partial(assemble_kernel, shifts, firsts, cycle, split),
        out_shape=jax.ShapeDtypeStruct(out_shape, F32),
        in_specs=[pl.BlockSpec(memory_space=pltpu.SMEM)] + [anywhere] * len(chunks),
        out_specs=anywhere,
        scratch_shapes=[
            pltpu.VMEM((2,) + shape, BF16),
            pltpu.VMEM((2,) + shape, F32),
            pltpu.SemaphoreType.DMA((2,)),
            pltpu.SemaphoreType.DMA((2,)),
        ],
        compiler_params=pltpu.CompilerParams(vmem_limit_bytes=16 << 20),
        cost_estimate=pl.CostEstimate(
            flops=cycle * math.prod(shape),
            bytes_accessed=6 * cycle * math.prod(shape),
            transcendentals=0,
        ),
        name=name,
    )(place[None], *chunks)


def ring_total(block):
    size = lax.axis_size("ctx")
    bits = 1
    while bits < size:
        block = block + lax.ppermute(block, "ctx", [(i, i ^ bits) for i in range(size)])
        bits *= 2
    return block


def after(block, *others):
    return lax.optimization_barrier((block,) + others)[0]


def rotary_tables(places):
    halfway = ROT // 2
    frequency = jnp.exp(
        jnp.arange(halfway, dtype=F32) * (-2.0 * math.log(10000.0) / ROT)
    )
    angles = places.astype(F32)[:, None] * frequency[None, :]
    cosine, sine = jnp.cos(angles), jnp.sin(angles)
    rest = (places.shape[0], LANES - ROT)
    return (
        jnp.concatenate([cosine, cosine, jnp.ones(rest, F32)], axis=1),
        jnp.concatenate([-sine, sine, jnp.zeros(rest, F32)], axis=1),
    )


def rotated(head, cosine, sine):
    halfway = ROT // 2
    lane = lax.broadcasted_iota(jnp.int32, head.shape, 1)
    swapped = jnp.where(
        lane < halfway,
        pltpu.roll(head, LANES - halfway, 1),
        pltpu.roll(head, halfway, 1),
    )
    return head * cosine + swapped * sine


def qkv_kernel(turns, x_ref, w_ref, b_ref, cos_ref, sin_ref, out_ref):
    turn = turns[pl.program_id(0)] > 0
    rows = x_ref[pl.program_id(1)]
    mixed = jnp.dot(rows, w_ref[...], preferred_element_type=F32) + b_ref[...].astype(F32)

    @pl.when(turn)
    def _():
        out_ref[:, :LANES] = rotated(mixed[:, :LANES], cos_ref[...], sin_ref[...]).astype(BF16)

    @pl.when(jnp.logical_not(turn))
    def _():
        out_ref[:, :LANES] = mixed[:, :LANES].astype(BF16)

    out_ref[:, LANES:] = mixed[:, LANES:].astype(BF16)


def qkv_slots(normed, weight, bias, cosine, sine, turns):
    seqs, tokens, width = normed.shape
    slots = weight.shape[1] // HEAD
    return pl.pallas_call(
        qkv_kernel,
        out_shape=jax.ShapeDtypeStruct((seqs, slots, tokens, HEAD), BF16),
        grid_spec=pltpu.PrefetchScalarGridSpec(
            num_scalar_prefetch=1,
            grid=(slots, seqs),
            in_specs=[
                pl.BlockSpec((seqs, tokens, width), lambda j, s, t: (0, 0, 0)),
                pl.BlockSpec((width, HEAD), lambda j, s, t: (0, j)),
                pl.BlockSpec((1, HEAD), lambda j, s, t: (0, j)),
                pl.BlockSpec((tokens, LANES), lambda j, s, t: (0, 0)),
                pl.BlockSpec((tokens, LANES), lambda j, s, t: (0, 0)),
            ],
            out_specs=pl.BlockSpec((None, None, tokens, HEAD), lambda j, s, t: (s, j, 0, 0)),
        ),
        compiler_params=pltpu.CompilerParams(vmem_limit_bytes=24 << 20),
        cost_estimate=pl.CostEstimate(
            flops=2 * seqs * tokens * width * slots * HEAD,
            bytes_accessed=2 * (normed.size + weight.size + seqs * slots * tokens * HEAD),
            transcendentals=0,
        ),
        name="qkv_slots",
    )(turns, normed, weight, bias[None, :], cosine, sine)


TILE = 256


def attention_kernel(
    runs,
    qkv_ref,
    go_ref,
    cos_ref,
    sin_ref,
    att_ref,
    grad_ref,
    q_s,
    k_s,
    v_s,
    go_s,
    dq_s,
    dk_s,
    dv_s,
    prob_s,
    att_s,
):
    count_runs = runs.shape[0]
    run_len = q_s.shape[0] // count_runs
    tiles = q_s.shape[0] // TILE
    scale = HEAD ** (-0.5)
    per_block = qkv_ref.shape[2] // run_len

    def place(index):
        block, part = index // per_block, lax.rem(index, per_block)
        inner = pl.ds(pl.multiple_of(part * run_len, run_len), run_len)
        outer = pl.ds(pl.multiple_of(runs[index] * run_len, run_len), run_len)
        return block, inner, outer

    @pl.loop(0, count_runs)
    def _(index):
        block, inner, outer = place(index)
        q_s[outer, :] = qkv_ref[block, 0, inner, :]
        k_s[outer, :] = qkv_ref[block, 1, inner, :]
        v_s[outer, :] = qkv_ref[block, 2, inner, :]
        go_s[outer, :] = go_ref[block, inner, :]

    dk_s[...] = jnp.zeros_like(dk_s)
    dv_s[...] = jnp.zeros_like(dv_s)

    def rows_of(index):
        return pl.ds(pl.multiple_of(index * TILE, TILE), TILE)

    across = (((1,), (1,)), ((), ()))
    along = (((0,), (0,)), ((), ()))

    @pl.loop(0, tiles)
    def _(row):
        rows = rows_of(row)
        query = q_s[rows, :]
        grad_out = go_s[rows, :]

        def score(col, top):
            part = (
                lax.dot_general(query, k_s[rows_of(col), :], across, preferred_element_type=F32)
                * scale
            )
            below = lax.broadcasted_iota(jnp.int32, part.shape, 0)
            right = lax.broadcasted_iota(jnp.int32, part.shape, 1)
            part = jnp.where((col - row) * TILE + right <= below, part, -1e30)
            prob_s[col] = part
            return jnp.maximum(top, jnp.max(part, axis=1, keepdims=True))

        top = lax.fori_loop(0, row + 1, score, jnp.full((TILE, 1), -1e30, F32))

        def weigh(col, total):
            part = jnp.exp(prob_s[col] - top)
            prob_s[col] = part
            return total + jnp.sum(part, axis=1, keepdims=True)

        total = lax.fori_loop(0, row + 1, weigh, jnp.zeros((TILE, 1), F32))
        inverse = 1.0 / total

        def attend(col, summed):
            part = prob_s[col] * inverse
            prob_s[col] = part
            return summed + jnp.dot(
                part.astype(BF16), v_s[rows_of(col), :], preferred_element_type=F32
            )

        attended = lax.fori_loop(0, row + 1, attend, jnp.zeros((TILE, HEAD), F32))
        att_s[rows, :] = attended.astype(BF16)
        delta = jnp.sum(attended * grad_out.astype(F32), axis=1, keepdims=True)

        def back(col, grad_query):
            cols = rows_of(col)
            prob = prob_s[col]
            grad_prob = lax.dot_general(
                grad_out, v_s[cols, :], across, preferred_element_type=F32
            )
            grad_score = (prob * (grad_prob - delta)).astype(BF16)
            dv_s[cols, :] += lax.dot_general(
                prob.astype(BF16), grad_out, along, preferred_element_type=F32
            )
            dk_s[cols, :] += lax.dot_general(
                grad_score, query, along, preferred_element_type=F32
            )
            return grad_query + jnp.dot(grad_score, k_s[cols, :], preferred_element_type=F32)

        dq_s[rows, :] = lax.fori_loop(0, row + 1, back, jnp.zeros((TILE, HEAD), F32))

    @pl.loop(0, count_runs)
    def _(index):
        block, inner, outer = place(index)
        cosine, sine = cos_ref[outer, :], -sin_ref[outer, :]
        att_ref[block, inner, :] = att_s[outer, :]
        for which, source in ((0, dq_s), (1, dk_s)):
            grad_ref[block, which, inner, :LANES] = rotated(
                source[outer, :LANES] * scale, cosine, sine
            ).astype(BF16)
            grad_ref[block, which, inner, LANES:] = (source[outer, LANES:] * scale).astype(BF16)
        grad_ref[block, 2, inner, :] = dv_s[outer, :].astype(BF16)


def attention_one_head(qkv, grad_out, runs, cosine, sine):
    blocks, _, tokens, _ = qkv.shape
    length = blocks * tokens
    return pl.pallas_call(
        attention_kernel,
        out_shape=(
            jax.ShapeDtypeStruct(grad_out.shape, BF16),
            jax.ShapeDtypeStruct(qkv.shape, BF16),
        ),
        in_specs=[
            pl.BlockSpec(memory_space=pltpu.SMEM),
            pl.BlockSpec(memory_space=pltpu.VMEM),
            pl.BlockSpec(memory_space=pltpu.VMEM),
            pl.BlockSpec(memory_space=pltpu.VMEM),
            pl.BlockSpec(memory_space=pltpu.VMEM),
        ],
        out_specs=(
            pl.BlockSpec(memory_space=pltpu.VMEM),
            pl.BlockSpec(memory_space=pltpu.VMEM),
        ),
        scratch_shapes=[
            pltpu.VMEM((length, HEAD), BF16),
            pltpu.VMEM((length, HEAD), BF16),
            pltpu.VMEM((length, HEAD), BF16),
            pltpu.VMEM((length, HEAD), BF16),
            pltpu.VMEM((length, HEAD), F32),
            pltpu.VMEM((length, HEAD), F32),
            pltpu.VMEM((length, HEAD), F32),
            pltpu.VMEM((length // TILE, TILE, TILE), F32),
            pltpu.VMEM((length, HEAD), BF16),
        ],
        compiler_params=pltpu.CompilerParams(vmem_limit_bytes=40 << 20),
        cost_estimate=pl.CostEstimate(
            flops=7 * length * length * HEAD,
            bytes_accessed=2 * (2 * qkv.size + 2 * grad_out.size),
            transcendentals=length * length // 2,
        ),
        name="attention_one_head",
    )(runs, qkv, grad_out, cosine, sine)


def attention_by_head(slots, grad_att, positions, place_of_block):
    tokens = slots.shape[1]
    blocks = lax.axis_size("ctx")
    run_len = tokens // 2
    send = jnp.transpose(slots.reshape(3, HEADS, tokens, HEAD), (1, 0, 2, 3))
    qkv = lax.all_to_all(send, "ctx", split_axis=0, concat_axis=0, tiled=True)
    go_send = jnp.transpose(grad_att.reshape(tokens, HEADS, HEAD), (1, 0, 2))
    go = lax.all_to_all(go_send, "ctx", split_axis=0, concat_axis=0, tiled=True)
    runs = positions.reshape(2 * blocks, run_len)[:, 0] // run_len
    cosine, sine = rotary_tables(jnp.arange(blocks * tokens, dtype=jnp.int32))
    att, grads = attention_one_head(qkv, go, runs, cosine, sine)
    grads = lax.all_to_all(grads, "ctx", split_axis=0, concat_axis=0, tiled=True)
    att = lax.all_to_all(att, "ctx", split_axis=0, concat_axis=0, tiled=True)
    attended = jnp.transpose(att, (1, 0, 2)).reshape(tokens, HEADS * HEAD)
    grad_slots = jnp.transpose(grads, (1, 0, 2, 3)).reshape(3 * HEADS, tokens, HEAD)
    return attended, grad_slots


def rotate_back(tensor, cosine, sine_table):
    halfway = ROT // 2
    first_part = tensor[..., :halfway]
    second_part = tensor[..., halfway:ROT]
    return jnp.concatenate(
        [
            first_part * cosine + second_part * sine_table,
            second_part * cosine - first_part * sine_table,
            tensor[..., ROT:],
        ],
        axis=-1,
    )


def attention_by_ring(slots, grad_att, positions, places):
    tokens = slots.shape[1]
    width = HEADS * HEAD
    cycle_size = lax.axis_size("ctx")
    my_index = lax.axis_index("ctx")
    score_scale = HEAD ** (-0.5)
    head_shape = (tokens, HEADS, HEAD)
    rows = jnp.transpose(slots.reshape(3, HEADS, tokens, HEAD), (0, 2, 1, 3))
    queries, key_rows, value_rows = rows[0], rows[1], rows[2]
    grad_att = grad_att.reshape(head_shape)
    key_heads = lax.all_gather(key_rows, "ctx", axis=0, tiled=True)
    value_heads = lax.all_gather(value_rows, "ctx", axis=0, tiled=True)
    scores = jnp.einsum("qhd,khd->qhk", queries, key_heads, preferred_element_type=F32)
    visible = positions[None, None, :] <= places[:, None, None]
    scores = jnp.where(visible, scores * score_scale, -1e30)
    top = jnp.max(scores, axis=-1)
    weights = jnp.where(visible, jnp.exp(scores - top[..., None]), 0.0)
    total = jnp.sum(weights, axis=-1)
    summed = jnp.einsum(
        "qhk,khd->qhd", weights.astype(BF16), value_heads, preferred_element_type=F32
    )
    attended_full = summed / total[..., None]
    log_total = top + jnp.log(total)
    row_delta = jnp.sum(grad_att.astype(F32) * attended_full, axis=-1)

    def pass_on(block):
        route = [(i, (i + 1) % cycle_size) for i in range(cycle_size)]
        return lax.ppermute(block, "ctx", route)

    def back_step(step_index, carried):
        key_block, value_block, grad_key, grad_value, grad_query = carried
        source = jnp.mod(my_index - step_index, cycle_size)
        key_places = lax.dynamic_slice_in_dim(positions, source * tokens, tokens)
        scores = (
            jnp.einsum("qhd,khd->qhk", queries, key_block, preferred_element_type=F32)
            * score_scale
        )
        visible = key_places[None, None, :] <= places[:, None, None]
        probs = jnp.where(visible, jnp.exp(scores - log_total[..., None]), 0.0)
        grad_value = grad_value + jnp.einsum(
            "qhk,qhd->khd", probs.astype(BF16), grad_att, preferred_element_type=F32
        )
        grad_probs = jnp.einsum(
            "qhd,khd->qhk", grad_att, value_block, preferred_element_type=F32
        )
        grad_scores = (probs * (grad_probs - row_delta[..., None])).astype(BF16)
        grad_query = (
            grad_query
            + jnp.einsum("qhk,khd->qhd", grad_scores, key_block, preferred_element_type=F32)
            * score_scale
        )
        grad_key = (
            grad_key
            + jnp.einsum("qhk,qhd->khd", grad_scores, queries, preferred_element_type=F32)
            * score_scale
        )
        return (
            pass_on(key_block),
            pass_on(value_block),
            pass_on(grad_key.astype(BF16)).astype(F32),
            pass_on(grad_value.astype(BF16)).astype(F32),
            grad_query,
        )

    zero = jnp.zeros(head_shape, F32)
    state = lax.fori_loop(0, cycle_size, back_step, (key_rows, value_rows, zero, zero, zero))
    halfway = ROT // 2
    frequency = jnp.exp(
        jnp.arange(halfway, dtype=F32) * (-2.0 * math.log(10000.0) / ROT)
    )
    angles = places.astype(F32)[:, None, None] * frequency
    cosine, sine = jnp.cos(angles), jnp.sin(angles)
    grads = jnp.stack(
        [rotate_back(state[4], cosine, sine), rotate_back(state[2], cosine, sine), state[3]]
    )
    grad_slots = jnp.transpose(grads.astype(BF16), (0, 2, 1, 3))
    attended = attended_full.astype(BF16).reshape(tokens, width)
    return attended, grad_slots.reshape(3 * HEADS, tokens, HEAD)


def shards(
    hidden_states,
    positions,
    ln1_gain,
    ln1_bias,
    ln2_gain,
    ln2_bias,
    qkv_weight,
    qkv_bias,
    out_weight,
    out_bias,
    up_weight,
    up_bias,
    down_weight,
    down_bias,
    grad_output,
):
    _, tokens, width = hidden_states.shape
    ranks = lax.axis_size("fsdp")
    cycle = lax.axis_size("ctx")
    mine = lax.axis_index("fsdp")
    column = lax.axis_index("ctx")
    place = ring_place()
    group = ranks * tokens
    slots_here = qkv_weight.shape[1] // HEAD
    own_cols = out_weight.shape[1]
    own_ff = up_weight.shape[1]

    def rank(bits):
        return jnp.bitwise_xor(mine, bits)

    x_own = hidden_states[0]
    norm_pieces = gather_by_partner(jnp.stack([ln1_gain, ln1_bias, ln2_gain, ln2_bias]))
    norm_params = jnp.zeros((4, width), BF16)
    for bits in range(ranks):
        norm_params = lax.dynamic_update_slice_in_dim(
            norm_params, norm_pieces[bits], rank(bits) * own_cols, 1
        )
    norm_params = norm_params.astype(F32)
    gain_one, shift_one, gain_two, shift_two = (norm_params[i] for i in range(4))
    x_all = gather_by_partner(x_own)
    g_all = gather_by_partner(grad_output[0])
    g_rows = g_all.reshape(group, width)

    def normalized(rows):
        rows = rows.astype(F32)
        offsets = rows - jnp.mean(rows, axis=-1, keepdims=True)
        spread = jnp.mean(offsets * offsets, axis=-1, keepdims=True)
        inverse = lax.rsqrt(spread + EPSILON)
        return offsets * inverse, inverse

    normal, _ = normalized(x_all.reshape(group, width))
    normed_one = (normal * gain_one + shift_one).astype(BF16)
    normed_two = (normal * gain_two + shift_two).astype(BF16)

    places = lax.dynamic_slice_in_dim(positions, column * tokens, tokens)
    cosine, sine = rotary_tables(places)
    turns = (mine * slots_here + jnp.arange(slots_here) < 2 * HEADS).astype(jnp.int32)
    pieces = qkv_slots(
        normed_one.reshape(ranks, tokens, width), qkv_weight, qkv_bias, cosine, sine, turns
    )
    pieces = [pieces[k] for k in range(ranks)]
    slots = jnp.zeros((3 * HEADS, tokens, HEAD), BF16)
    for bits, piece in enumerate(exchange_by_partner(pieces)):
        slots = lax.dynamic_update_slice_in_dim(slots, piece, rank(bits) * slots_here, 0)

    g_cols = lax.dynamic_slice_in_dim(g_rows, mine * own_cols, own_cols, axis=1)
    att_part = jnp.einsum("te,de->td", g_cols, out_weight, preferred_element_type=F32)
    grad_att = scatter_sum_by_partner(att_part.reshape(ranks, tokens, width)).astype(BF16)

    up_in = jnp.dot(normed_two, up_weight, preferred_element_type=F32) + up_bias.astype(F32)
    below = 0.5 * (1.0 + lax.erf(up_in * INV_ROOT_TWO))
    activated = (up_in * below).astype(BF16)
    slope = below + up_in * jnp.exp(-0.5 * up_in * up_in) * INV_ROOT_TAU

    def chunk_cols(array, index):
        step = array.shape[1] // cycle
        return lax.dynamic_slice_in_dim(array, index * step, step, axis=1)

    def product(left, right):
        return lambda index: jnp.einsum(
            "tc,tj->cj", chunk_cols(left, index), right, preferred_element_type=F32
        )

    down_piece = ring_sum(product(activated, g_rows), place).astype(BF16)
    swapped = exchange_by_partner(
        [
            lax.dynamic_slice_in_dim(down_piece, rank(k) * own_cols, own_cols, axis=1)
            for k in range(ranks)
        ]
    )
    down_own = jnp.zeros((ranks,) + swapped[0].shape, BF16)
    for bits, piece in enumerate(swapped):
        down_own = lax.dynamic_update_slice_in_dim(down_own, piece[None], rank(bits), 0)

    down_weight = after(down_weight, *pieces)
    row_pieces = exchange_by_partner(
        [
            lax.dynamic_slice_in_dim(down_weight, rank(k) * own_ff, own_ff, axis=0)
            for k in range(ranks)
        ]
    )
    down_rows = jnp.zeros((own_ff, width), BF16)
    for bits, piece in enumerate(row_pieces):
        down_rows = lax.dynamic_update_slice_in_dim(down_rows, piece, rank(bits) * own_cols, 1)

    grad_act = jnp.einsum("td,fd->tf", g_rows, down_rows, preferred_element_type=F32)
    grad_up = (grad_act * slope).astype(BF16)
    up_own = ring_sum(product(normed_two, grad_up), place).astype(BF16)
    hidden_two = jnp.einsum("tf,cf->tc", grad_up, up_weight, preferred_element_type=F32)
    mlp_part = jnp.dot(activated, down_rows, preferred_element_type=F32)

    if cycle == HEADS:
        attended, grad_slots = attention_by_head(slots, grad_att, positions, place)
    else:
        attended, grad_slots = attention_by_ring(slots, grad_att, positions, places)

    att_rows = gather_by_partner(attended).reshape(group, width)
    att_result = jnp.dot(att_rows, out_weight, preferred_element_type=F32) + (
        out_bias.astype(F32) + down_bias.astype(F32)
    )
    some = lax.dynamic_slice_in_dim(mlp_part, mine * own_cols, own_cols, axis=1)
    out_part = lax.dynamic_update_slice_in_dim(
        mlp_part, some + att_result, mine * own_cols, axis=1
    )
    total = scatter_sum_by_partner(out_part.reshape(ranks, tokens, width))
    output = (x_own.astype(F32) + total).astype(BF16)[None]
    out_own = ring_sum(product(att_rows, g_cols), place).astype(BF16)

    back_pieces = exchange_by_partner(
        [
            lax.dynamic_slice_in_dim(grad_slots, rank(k) * slots_here, slots_here, axis=0)
            for k in range(ranks)
        ]
    )
    grad_mixed = jnp.transpose(jnp.stack(back_pieces), (0, 2, 1, 3)).reshape(
        group, slots_here * HEAD
    )
    qkv_own = ring_sum(product(normed_one, grad_mixed), place).astype(BF16)
    hidden_one = jnp.einsum("tj,cj->tc", grad_mixed, qkv_weight, preferred_element_type=F32)

    both = (hidden_one * gain_one + hidden_two * gain_two).reshape(ranks, tokens, width)
    scaled = scatter_sum_by_partner(both)
    normal_own, inverse_own = normalized(x_own)
    grad_x = inverse_own * (
        scaled
        - jnp.mean(scaled, axis=-1, keepdims=True)
        - normal_own * jnp.mean(scaled * normal_own, axis=-1, keepdims=True)
    )
    grad_input = (grad_output[0].astype(F32) + grad_x).astype(BF16)[None]

    norm_sums = jnp.stack(
        [
            jnp.sum(hidden_one * normal, axis=0),
            jnp.sum(hidden_one, axis=0),
            jnp.sum(hidden_two * normal, axis=0),
            jnp.sum(hidden_two, axis=0),
        ]
    )
    norm_sums = lax.optimization_barrier(norm_sums)
    blocks = jnp.stack(
        [
            lax.dynamic_slice_in_dim(norm_sums, rank(k) * own_cols, own_cols, axis=1)
            for k in range(ranks)
        ]
    )
    beside = partner(jnp.stack([blocks[1], blocks[3]]), 1)
    across = partner(blocks[2] + beside[1], 2)
    norm_sums = blocks[0] + beside[0] + across
    sums = ring_total(
        jnp.concatenate(
            [
                norm_sums.reshape(-1),
                jnp.sum(grad_mixed.astype(F32), axis=0),
                jnp.sum(grad_up.astype(F32), axis=0),
                jnp.sum(g_cols.astype(F32), axis=0),
            ]
        )
    )
    norm_sums, sums = sums[: 4 * own_cols].reshape(4, own_cols), sums[4 * own_cols :]
    edge = qkv_bias.shape[0]
    g_qkv_bias = sums[:edge]
    g_up_bias = sums[edge : edge + own_ff]
    g_out_bias = sums[edge + own_ff :]

    g_down = assemble(ring_spread(down_own), place, "assemble_down")
    g_down = g_down.reshape(down_weight.shape)
    g_up = assemble(ring_spread(up_own), place, "assemble_up").reshape(up_weight.shape)
    g_out = assemble(ring_spread(out_own), place, "assemble_out").reshape(out_weight.shape)
    g_qkv = assemble(ring_spread(qkv_own), place, "assemble_qkv").reshape(qkv_weight.shape)

    return (
        output,
        grad_input,
        norm_sums[0],
        norm_sums[1],
        norm_sums[2],
        norm_sums[3],
        g_qkv,
        g_qkv_bias,
        g_out,
        g_out_bias,
        g_up,
        g_up_bias,
        g_down,
        g_out_bias,
    )


def solution(mesh):
    vector, matrix, rows = P("fsdp"), P(None, "fsdp"), P("fsdp", "ctx", None)
    return jax.shard_map(
        shards,
        mesh=mesh,
        in_specs=(
            rows,
            P(),
            vector,
            vector,
            vector,
            vector,
            matrix,
            vector,
            matrix,
            vector,
            matrix,
            vector,
            matrix,
            vector,
            rows,
        ),
        out_specs=(
            rows,
            rows,
            vector,
            vector,
            vector,
            vector,
            matrix,
            vector,
            matrix,
            vector,
            matrix,
            vector,
            matrix,
            vector,
        ),
        check_vma=False,
    )
```
